32 devices in a mesh: ctx: 8 (over y, x, core), wa: 4 (over z).
Axes of the slice: x: 2, y: 2, z: 4, core: 2. Of those that a mesh axis runs over, the one named last changes fastest.
Arguments:
- tokens: bfloat16 [8, 1024, 768], P('wa', 'ctx'), may hold values from -6 to 6
- doc_lengths: int32 [8], replicated, may hold values from 256 to 1024, as said below
- group_deal: int32 [8, 8], replicated, may hold values from 0 to 7, each once within a row
- qkv_weight: bfloat16 [768, 2304], P('wa'), may hold values from -0.21875 to 0.21875
- out_weight: bfloat16 [768, 768], P('wa'), may hold values from -2.5 to 2.5
- up_weight: bfloat16 [768, 3072], P('wa'), may hold values from -0.21875 to 0.21875
- up_bias: bfloat16 [3072], P('wa'), may hold values from -3 to 3
- down_weight: bfloat16 [3072, 768], P('wa'), may hold values from -0.109375 to 0.109375
- proj_weight: bfloat16 [768, 128], P('wa'), may hold values from -0.21875 to 0.21875
- vectors: bfloat16 [8, 768], P(None, 'wa'), may hold values from -2 to 2
- cotangent: bfloat16 [8, 1024, 128], P('wa', 'ctx'), may hold values from -6 to 6
Outputs:
- embeddings: bfloat16 [8, 1024, 128], P('wa', 'ctx')
- tokens_grad: float32 [8, 1024, 768], P('wa', 'ctx')
- qkv_grad: float32 [768, 2304], P('wa')
- out_grad: float32 [768, 768], P('wa')
- up_grad: float32 [768, 3072], P('wa')
- bias_grad: float32 [3072], P('wa')
- down_grad: float32 [3072, 768], P('wa')
- proj_grad: float32 [768, 128], P('wa')
- vectors_grad: float32 [8, 768], P(None, 'wa')
The draws below stay inside these ranges and needn't reach their ends.
Inputs may be any that keep to these rules, and one draw needn't show every extreme that they name: `doc_lengths`: every draw has a sequence with all 1024 slots valid. `group_deal`: each row is a permutation of the block numbers of a sequence.
All inputs are finite; a program needn't handle non-finite values.
Results may differ from the reference program's by a relative error of at most 0.023.
Values may be sent and summed in bfloat16 or wider, within the bound.
No kernel may reach another device: no remote copies, remote signals or barrier semaphores. Data moves between devices by JAX's collectives and lax.ppermute only.
A program may use at most 256 MiB of HBM per device.

```python
import jax
import jax.numpy as jnp
from jax import lax

D = 768
H = 12
HEAD = 64
FF = 3072
E = 128
GROUP = 128
SEQ_LEN = 1024
NSEQ = 8
N_CTX = 8


def draw_doc_lengths(key, part):
    first, second = jax.random.split(key)
    drawn = jax.random.randint(first, (NSEQ,), SEQ_LEN // 4, SEQ_LEN + 1)
    chosen = jax.random.randint(second, (), 0, NSEQ)
    return jnp.where(jnp.arange(NSEQ) == chosen, SEQ_LEN, drawn).astype(jnp.int32)


def draw_vectors(key, part):
    first, second = jax.random.split(key)
    shifts = jnp.clip(0.45 * jax.random.normal(first, (8, D)), -2.0, 2.0)
    gains = jnp.exp(jax.random.uniform(second, (8, D), minval=-0.5, maxval=0.5))
    rows_index = jnp.arange(8)
    is_gain = (rows_index == 3) | (rows_index == 6)
    return jnp.where(is_gain[:, None], gains, shifts).astype(jnp.float32).astype(jnp.bfloat16)


def block_scale(stream_key, dims, cuts, low, high):
    loudness = 1.0
    for dim, parts in cuts:
        steps = jax.random.uniform(jax.random.fold_in(jax.random.fold_in(stream_key, 6), dim), (parts,), jnp.float32, low / len(cuts), high / len(cuts))
        loudness = loudness * jnp.repeat(jnp.exp(steps), dims[dim] // parts).reshape((-1,) + (1,) * (len(dims) - 1 - dim))
    return loudness


def normal_values(own_key, shape, scale, limit, cuts=(), held_as=jnp.bfloat16):
    gain = block_scale(own_key, shape, cuts, -0.22, 0.18) if cuts else 1.0
    values = jax.random.normal(own_key, shape, jnp.float32) * scale * gain
    return jnp.minimum(jnp.maximum(values, -limit), limit).astype(held_as)


def setup_inputs(seed: int = 0) -> dict:
    streams_of = jax.random.split(jax.random.key(seed), 12)
    return {
        "tokens": normal_values(streams_of[0], (NSEQ, SEQ_LEN, D), 1.0, 6.0, ((0, 4), (1, 8))),
        "doc_lengths": draw_doc_lengths(jax.random.fold_in(streams_of[11], 71), 0),
        "group_deal": jax.vmap(lambda own: jax.random.permutation(own, N_CTX))(jax.random.split(streams_of[2], NSEQ)).reshape((NSEQ, N_CTX)).astype(jnp.int32),
        "qkv_weight": normal_values(streams_of[3], (D, 3 * D), D ** -0.5, 0.21875, ((0, 4),)),
        "out_weight": normal_values(streams_of[4], (D, D), (max(1, D * 8 // SEQ_LEN)) ** -0.5, 2.5, ((0, 4),)),
        "up_weight": normal_values(streams_of[5], (D, FF), D ** -0.5, 0.21875, ((0, 4),)),
        "up_bias": normal_values(streams_of[6], (FF,), 0.5, 3.0, ((0, 4),)),
        "down_weight": normal_values(streams_of[7], (FF, D), FF ** -0.5, 0.109375, ((0, 4),)),
        "proj_weight": normal_values(streams_of[8], (D, E), D ** -0.5, 0.21875, ((0, 4),)),
        "vectors": draw_vectors(jax.random.fold_in(streams_of[11], 71), 0),
        "cotangent": normal_values(streams_of[10], (NSEQ, SEQ_LEN, E), 1.0, 6.0, ((0, 4), (1, 8))),
    }


NEG_FILL = -1e+30
NORM_EPS = 1e-06
ROOT_HALF = 0.7071067811865476
HIGHEST_MODE = lax.Precision.HIGHEST

@jax.custom_vjp
def low(v):
    return lax.optimization_barrier(v.astype(jnp.bfloat16)).astype(jnp.float32)

@jax.custom_vjp
def low_back(v):
    return v

def low_keep(v):
    return (low(v), None)

def low_pass(kept, grad):
    return (grad,)

def back_keep(v):
    return (v, None)

def back_low(kept, grad):
    return (low(grad),)
low.defvjp(low_keep, low_pass)
low_back.defvjp(back_keep, back_low)

def layer_norm(inputs, gain_row, shift_row):
    middle = lax.optimization_barrier(jnp.mean(inputs, axis=-1, keepdims=True))
    center = inputs - middle
    spread = lax.optimization_barrier(jnp.mean(center * center, axis=-1, keepdims=True))
    return center * lax.rsqrt(spread + NORM_EPS) * gain_row + shift_row

def matmul(left_side, right_side):
    return jnp.dot(left_side, right_side, precision=HIGHEST_MODE)

def one_sequence(params, hidden, valid_row):
    qkv_weight, out_weight, up_weight, up_bias, down_weight, proj_weight, vectors = params
    seq_span = hidden.shape[0]
    mixed = matmul(hidden, qkv_weight)
    queries = low(low_back((mixed[:, :D] + vectors[0]) * HEAD ** (-0.5)))
    keys_all = low(low_back(mixed[:, D:2 * D]))
    values_all = low(low_back(mixed[:, 2 * D:] + vectors[1]))
    key_heads = keys_all.reshape(seq_span, H, HEAD)
    value_heads = values_all.reshape(seq_span, H, HEAD)
    tile_width = 512 if seq_span % 512 == 0 else seq_span

    def attend(query_tile):
        scores = low_back(jnp.einsum('qhd,khd->hqk', query_tile, key_heads, precision=HIGHEST_MODE))
        scores = jnp.where(valid_row[None, None, :], scores, NEG_FILL)
        highest = lax.optimization_barrier(jnp.max(scores, axis=-1, keepdims=True))
        raised = jnp.exp(scores - highest)
        probs = low(raised / lax.optimization_barrier(jnp.sum(raised, axis=-1, keepdims=True)))
        return jnp.einsum('hqk,khd->qhd', probs, value_heads, precision=HIGHEST_MODE)
    attended = lax.map(jax.checkpoint(attend), queries.reshape(seq_span // tile_width, tile_width, H, HEAD))
    attended = low(low_back(attended.reshape(seq_span, D)))
    first_sum = hidden + (low_back(matmul(attended, out_weight)) + vectors[2])
    normed = layer_norm(first_sum, vectors[3], vectors[4])
    inner_sum = low_back(matmul(low(normed), up_weight)) + up_bias
    active = low(0.5 * inner_sum * (1.0 + lax.erf(inner_sum * ROOT_HALF)))
    second_sum = normed + (low_back(matmul(active, down_weight)) + vectors[5])
    final_sum = layer_norm(second_sum, vectors[6], vectors[7])
    project = low_back(matmul(low(final_sum), proj_weight))
    scaling = lax.rsqrt(lax.optimization_barrier(jnp.sum(project * project, axis=-1, keepdims=True)) + NORM_EPS)
    return project * scaling * valid_row[:, None].astype(project.dtype)

def reference(tokens, doc_lengths, group_deal, qkv_weight, out_weight, up_weight, up_bias, down_weight, proj_weight, vectors, cotangent):
    offsets = jnp.tile(jnp.arange(GROUP, dtype=jnp.int32), N_CTX)
    positions = jnp.repeat(group_deal.astype(jnp.int32), GROUP, axis=1) * GROUP + offsets[None, :]
    valid = positions < doc_lengths.astype(jnp.int32)[:, None]
    floats = tuple((member.astype(jnp.float32) for member in (tokens, qkv_weight, out_weight, up_weight, up_bias, down_weight, proj_weight, vectors)))

    def forward(hidden_all, *params):

        def per_sequence(paired):
            return one_sequence(params, paired[0], paired[1])
        return lax.map(jax.checkpoint(per_sequence), (hidden_all, valid))
    embedded, pullback = jax.vjp(forward, *floats)
    gradients = pullback(cotangent.astype(jnp.float32))
    return (embedded.astype(jnp.bfloat16), gradients[0], gradients[1], gradients[2], gradients[3], gradients[4], gradients[5], gradients[6], gradients[7])
```

```python
from functools import partial

import jax
import jax.numpy as jnp
from jax import lax
from jax.experimental import pallas as pl
from jax.experimental.pallas import tpu as pltpu
from jax.sharding import PartitionSpec as P

H = 12
HEAD = 64


NEG_FILL = -1e30
NORM_EPS = 1e-06
ROOT_HALF = 0.7071067811865476
DENSITY_SCALE = 0.3989422804014327


def norm_rows(inputs, gain_row, shift_row):
    middle = jnp.mean(inputs, axis=-1, keepdims=True)
    center = inputs - middle
    spread = jnp.mean(center * center, axis=-1, keepdims=True)
    scaled = lax.rsqrt(spread + NORM_EPS)
    unit_rows = center * scaled
    return (unit_rows * gain_row + shift_row, unit_rows, scaled)


def norm_back(grad_in, unit_rows, scaled, gain_row):
    gain_grad = jnp.sum(grad_in * unit_rows, axis=(0, 1))
    shift_grad = jnp.sum(grad_in, axis=(0, 1))
    inner_grad = grad_in * gain_row
    centered = inner_grad - jnp.mean(inner_grad, axis=-1, keepdims=True)
    result = scaled * (
        centered - unit_rows * jnp.mean(inner_grad * unit_rows, axis=-1, keepdims=True)
    )
    return (result, gain_grad, shift_grad)


def gelu_both(inner_sum):
    normal_cdf = 0.5 * (1.0 + lax.erf(inner_sum * ROOT_HALF))
    density = jnp.exp(-0.5 * inner_sum * inner_sum) * DENSITY_SCALE
    return (inner_sum * normal_cdf, normal_cdf + inner_sum * density)


def split_tiles(key_rows, value_rows, key_valid):
    key_count = key_rows.shape[0]
    tile_width = 512
    tile_count = key_count // tile_width
    return (
        key_rows.reshape(tile_count, tile_width, H, HEAD),
        value_rows.reshape(tile_count, tile_width, H, HEAD),
        key_valid.reshape(tile_count, tile_width),
    )


def masked_scores(queries, key_tile, mask_tile):
    products = jnp.einsum("qhd,khd->hqk", queries, key_tile, preferred_element_type=jnp.float32)
    return jnp.where(mask_tile[None, None, :], products, NEG_FILL)


def attend_forward(queries, key_rows, value_rows, key_valid):
    key_tiles, value_tiles, mask_tiles = split_tiles(key_rows, value_rows, key_valid)
    row_span = queries.shape[0]

    def stats_step(running, portion):
        highest, summed = running
        key_tile, mask_tile = portion
        scores = masked_scores(queries, key_tile, mask_tile)
        new_peak = jnp.maximum(highest, jnp.max(scores, axis=-1))
        raised = jnp.where(mask_tile[None, None, :], jnp.exp(scores - new_peak[:, :, None]), 0.0)
        return ((new_peak, summed * jnp.exp(highest - new_peak) + jnp.sum(raised, axis=-1)), None)

    start_peak = jnp.full((H, row_span), NEG_FILL, jnp.float32)
    start_sum = jnp.zeros((H, row_span), jnp.float32)
    (highest, summed), _ = lax.scan(stats_step, (start_peak, start_sum), (key_tiles, mask_tiles))
    logsum = highest + jnp.log(summed)

    def value_step(running, portion):
        key_tile, value_tile, mask_tile = portion
        scores = masked_scores(queries, key_tile, mask_tile)
        prob_low = jnp.where(
            mask_tile[None, None, :], jnp.exp(scores - logsum[:, :, None]), 0.0
        ).astype(jnp.bfloat16)
        return (
            running
            + jnp.einsum("hqk,khd->qhd", prob_low, value_tile, preferred_element_type=jnp.float32),
            None,
        )

    attended, _ = lax.scan(
        value_step,
        jnp.zeros((row_span, H, HEAD), jnp.float32),
        (key_tiles, value_tiles, mask_tiles),
    )
    return (attended, logsum)


def attend_backward(
    queries, key_rows, value_rows, key_valid, logsum, delta_rows, grad_heads, with_keys
):
    key_tiles, value_tiles, mask_tiles = split_tiles(key_rows, value_rows, key_valid)

    def back_step(running, portion):
        key_tile, value_tile, mask_tile = portion
        scores = masked_scores(queries, key_tile, mask_tile)
        prob_rows = jnp.where(mask_tile[None, None, :], jnp.exp(scores - logsum[:, :, None]), 0.0)
        prob_grad = jnp.einsum(
            "qhd,khd->hqk", grad_heads, value_tile, preferred_element_type=jnp.float32
        )
        score_low = (prob_rows * (prob_grad - delta_rows[:, :, None])).astype(jnp.bfloat16)
        running = running + jnp.einsum(
            "hqk,khd->qhd", score_low, key_tile, preferred_element_type=jnp.float32
        )
        value_part = jnp.einsum(
            "hqk,qhd->khd",
            prob_rows.astype(jnp.bfloat16),
            grad_heads,
            preferred_element_type=jnp.float32,
        )
        key_part = jnp.einsum(
            "hqk,qhd->khd", score_low, queries, preferred_element_type=jnp.float32
        )
        return (running, (key_part, value_part))

    start_grad = jnp.zeros(queries.shape, jnp.float32)
    query_grad, pieces = lax.scan(back_step, start_grad, (key_tiles, value_tiles, mask_tiles))
    key_count = key_rows.shape[0]
    return (
        query_grad,
        pieces[0].reshape(key_count, H * HEAD),
        pieces[1].reshape(key_count, H * HEAD),
    )


def body(
    tokens,
    doc_lengths,
    group_deal,
    qkv_weight,
    out_weight,
    up_weight,
    up_bias,
    down_weight,
    proj_weight,
    vectors,
    cotangent,
):
    gathered = (
        lax.all_gather(qkv_weight, "wa", axis=0, tiled=True),
        lax.all_gather(out_weight, "wa", axis=0, tiled=True),
        lax.all_gather(up_weight, "wa", axis=0, tiled=True),
        lax.all_gather(up_bias, "wa", axis=0, tiled=True),
        lax.all_gather(down_weight, "wa", axis=0, tiled=True),
        lax.all_gather(proj_weight, "wa", axis=0, tiled=True),
        lax.all_gather(vectors, "wa", axis=1, tiled=True),
    )
    qkv_full, out_full, up_full, bias_full, down_full, proj_full, vector_full = gathered
    seq_count, group_rows, model_width = tokens.shape
    ctx_count = lax.axis_size("ctx")
    seq_start = lax.axis_index("wa") * seq_count
    my_lengths = lax.dynamic_slice_in_dim(doc_lengths, seq_start, seq_count, 0)
    my_deal = lax.dynamic_slice_in_dim(group_deal, seq_start, seq_count, 0)
    offsets = jnp.tile(jnp.arange(group_rows, dtype=jnp.int32), ctx_count)
    positions = jnp.repeat(my_deal, group_rows, axis=1) * group_rows + offsets[None, :]
    key_valid = positions < my_lengths[:, None]
    query_valid = lax.dynamic_slice_in_dim(
        key_valid, lax.axis_index("ctx") * group_rows, group_rows, 1
    )
    row_mask = query_valid.astype(jnp.float32)[:, :, None]
    query_scale = HEAD ** (-0.5)
    mixed_rows = jnp.einsum("scd,de->sce", tokens, qkv_full, preferred_element_type=jnp.float32)
    queries = ((mixed_rows[:, :, :model_width] + vector_full[0]) * query_scale).astype(jnp.bfloat16)
    key_rows = mixed_rows[:, :, model_width : 2 * model_width].astype(jnp.bfloat16)
    value_rows = (mixed_rows[:, :, 2 * model_width :] + vector_full[1]).astype(jnp.bfloat16)
    all_keys, all_values = (
        lax.all_gather(key_rows, "ctx", axis=1, tiled=True),
        lax.all_gather(value_rows, "ctx", axis=1, tiled=True),
    )
    query_heads = queries.reshape(seq_count, group_rows, H, HEAD)
    attended, logsum = jax.vmap(attend_forward)(query_heads, all_keys, all_values, key_valid)
    attended_low = attended.reshape(seq_count, group_rows, model_width).astype(jnp.bfloat16)
    first_sum = tokens.astype(jnp.float32) + (
        jnp.einsum("scd,de->sce", attended_low, out_full, preferred_element_type=jnp.float32)
        + vector_full[2]
    )
    normed, unit_one, scale_one = norm_rows(first_sum, vector_full[3], vector_full[4])
    normed_low = normed.astype(jnp.bfloat16)
    inner_sum = (
        jnp.einsum("scd,df->scf", normed_low, up_full, preferred_element_type=jnp.float32)
        + bias_full
    )
    active, gelu_slope = gelu_both(inner_sum)
    active_low = active.astype(jnp.bfloat16)
    second_sum = normed + (
        jnp.einsum("scf,fd->scd", active_low, down_full, preferred_element_type=jnp.float32)
        + vector_full[5]
    )
    final_sum, unit_two, scale_two = norm_rows(second_sum, vector_full[6], vector_full[7])
    final_low = final_sum.astype(jnp.bfloat16)
    project = jnp.einsum("scd,de->sce", final_low, proj_full, preferred_element_type=jnp.float32)
    inverse = lax.rsqrt(jnp.sum(project * project, axis=-1, keepdims=True) + NORM_EPS)
    direction = project * inverse
    embeddings = (direction * row_mask).astype(jnp.bfloat16)
    upstream = cotangent.astype(jnp.float32) * row_mask
    project_grad = (
        inverse * (upstream - direction * jnp.sum(upstream * direction, axis=-1, keepdims=True))
    ).astype(jnp.bfloat16)
    proj_grad = jnp.einsum(
        "scd,sce->de", final_low, project_grad, preferred_element_type=jnp.float32
    )
    final_grad = jnp.einsum(
        "sce,de->scd", project_grad, proj_full, preferred_element_type=jnp.float32
    )
    second_grad, gain_two, shift_two = norm_back(final_grad, unit_two, scale_two, vector_full[6])
    down_low = second_grad.astype(jnp.bfloat16)
    down_grad = jnp.einsum("scf,scd->fd", active_low, down_low, preferred_element_type=jnp.float32)
    inner_grad = (
        jnp.einsum("scd,fd->scf", down_low, down_full, preferred_element_type=jnp.float32)
        * gelu_slope
    )
    bias_grad = jnp.sum(inner_grad, axis=(0, 1))
    inner_low = inner_grad.astype(jnp.bfloat16)
    up_grad = jnp.einsum("scd,scf->df", normed_low, inner_low, preferred_element_type=jnp.float32)
    normed_grad = second_grad + jnp.einsum(
        "scf,df->scd", inner_low, up_full, preferred_element_type=jnp.float32
    )
    first_grad, gain_one, shift_one = norm_back(normed_grad, unit_one, scale_one, vector_full[3])
    first_low = first_grad.astype(jnp.bfloat16)
    out_grad = jnp.einsum(
        "scd,sce->de", attended_low, first_low, preferred_element_type=jnp.float32
    )
    attended_grad = jnp.einsum(
        "sce,de->scd", first_low, out_full, preferred_element_type=jnp.float32
    ).astype(jnp.bfloat16)
    grad_heads = attended_grad.reshape(seq_count, group_rows, H, HEAD)
    delta_rows = jnp.sum(grad_heads.astype(jnp.float32) * attended, axis=-1)
    delta_heads = jnp.swapaxes(delta_rows, 1, 2)
    query_grad, key_terms, value_terms = jax.vmap(partial(attend_backward, with_keys=True))(
        query_heads, all_keys, all_values, key_valid, logsum, delta_heads, grad_heads
    )
    key_grad, value_grad = (
        lax.psum_scatter(
            key_terms.astype(jnp.bfloat16), "ctx", scatter_dimension=1, tiled=True
        ).astype(jnp.float32),
        lax.psum_scatter(
            value_terms.astype(jnp.bfloat16), "ctx", scatter_dimension=1, tiled=True
        ).astype(jnp.float32),
    )
    query_part = (
        query_grad.reshape(seq_count, group_rows, model_width).astype(jnp.bfloat16) * query_scale
    )
    value_part = value_grad.astype(jnp.bfloat16)
    mixed_grad = jnp.concatenate([query_part, key_grad.astype(jnp.bfloat16), value_part], axis=-1)
    qkv_grad = jnp.einsum("scd,sce->de", tokens, mixed_grad, preferred_element_type=jnp.float32)
    tokens_grad = first_grad + jnp.einsum(
        "sce,de->scd", mixed_grad, qkv_full, preferred_element_type=jnp.float32
    )
    vectors_grad = jnp.stack(
        [
            jnp.sum(query_part.astype(jnp.float32), axis=(0, 1)),
            jnp.sum(value_part.astype(jnp.float32), axis=(0, 1)),
            jnp.sum(first_grad, axis=(0, 1)),
            gain_one,
            shift_one,
            jnp.sum(second_grad, axis=(0, 1)),
            gain_two,
            shift_two,
        ],
        axis=0,
    )
    owned = (
        lax.psum_scatter(
            qkv_grad.astype(jnp.bfloat16), "wa", scatter_dimension=0, tiled=True
        ).astype(jnp.float32),
        lax.psum_scatter(
            out_grad.astype(jnp.bfloat16), "wa", scatter_dimension=0, tiled=True
        ).astype(jnp.float32),
        lax.psum_scatter(
            up_grad.astype(jnp.bfloat16), "wa", scatter_dimension=0, tiled=True
        ).astype(jnp.float32),
        lax.psum_scatter(
            bias_grad.astype(jnp.bfloat16), "wa", scatter_dimension=0, tiled=True
        ).astype(jnp.float32),
        lax.psum_scatter(
            down_grad.astype(jnp.bfloat16), "wa", scatter_dimension=0, tiled=True
        ).astype(jnp.float32),
        lax.psum_scatter(
            proj_grad.astype(jnp.bfloat16), "wa", scatter_dimension=0, tiled=True
        ).astype(jnp.float32),
        lax.psum_scatter(
            vectors_grad.astype(jnp.bfloat16), "wa", scatter_dimension=1, tiled=True
        ).astype(jnp.float32),
    )
    summed = (
        lax.psum(owned[0].astype(jnp.bfloat16), "ctx").astype(jnp.float32),
        lax.psum(owned[1].astype(jnp.bfloat16), "ctx").astype(jnp.float32),
        lax.psum(owned[2].astype(jnp.bfloat16), "ctx").astype(jnp.float32),
        lax.psum(owned[3].astype(jnp.bfloat16), "ctx").astype(jnp.float32),
        lax.psum(owned[4].astype(jnp.bfloat16), "ctx").astype(jnp.float32),
        lax.psum(owned[5].astype(jnp.bfloat16), "ctx").astype(jnp.float32),
        lax.psum(owned[6].astype(jnp.bfloat16), "ctx").astype(jnp.float32),
    )
    return (
        embeddings,
        tokens_grad,
        summed[0],
        summed[1],
        summed[2],
        summed[3],
        summed[4],
        summed[5],
        summed[6],
    )


def swap(value, axis, bit=1):
    size = lax.axis_size(axis)
    return lax.ppermute(value, axis, [(i, i ^ bit) for i in range(size)])


def grow(value, offsets, axis, bit, unit):
    return (
        jnp.concatenate([value, swap(value, axis, bit)], axis=0),
        offsets + [held ^ (bit * unit) for held in offsets],
    )


def pick(value, index):
    return lax.dynamic_index_in_dim(value, index, 0, keepdims=False)


def place_blocks(flip, pieces, cuts, plan):
    outs = []
    for (top, bottom, low, high), homes in zip(cuts, plan):
        outs.append(jax.ShapeDtypeStruct((len(homes) * (bottom - top), high - low), pieces[0].dtype))

    def kernel(flip_ref, *refs):
        piece_refs, out_refs = refs[: len(pieces)], refs[len(pieces) :]
        for which, out_ref in enumerate(out_refs):
            top, bottom, low, high = cuts[which]
            tall, block = bottom - top, 0
            for piece_ref in piece_refs:
                for inner in range(piece_ref.shape[0]):
                    home = jnp.bitwise_xor(flip_ref[which], plan[which][block])
                    start = pl.multiple_of(home * tall, tall)
                    out_ref[pl.ds(start, tall), :] = piece_ref[inner, top:bottom, low:high]
                    block += 1

    return pl.pallas_call(
        kernel,
        out_shape=tuple(outs),
        in_specs=[pl.BlockSpec(memory_space=pltpu.SMEM)]
        + [pl.BlockSpec(memory_space=pltpu.VMEM) for _ in pieces],
        name="place_blocks",
    )(flip, *pieces)


def head_lanes(head, wide):
    lane = lax.broadcasted_iota(jnp.int32, (1, wide), 1)
    return (lane >= head * HEAD) & (lane < (head + 1) * HEAD)


def attend_kernel(tokens_ref, weight_ref, rows_ref, mask_ref, att_ref, q_ref, k_ref, v_ref, lse_ref, *, heads):
    span = heads * HEAD
    wide = q_ref.shape[1]
    lane = lax.broadcasted_iota(jnp.int32, (1, wide), 1)
    rows = rows_ref[...].astype(jnp.float32)
    slots = tokens_ref.shape[0]
    query_scale = HEAD ** (-0.5)
    tokens = tokens_ref[...]
    k_mix = jnp.dot(tokens, weight_ref[:, wide : 2 * wide], preferred_element_type=jnp.float32)
    k_ref[...] = jnp.where(lane < span, k_mix, mask_ref[...].astype(jnp.float32)).astype(jnp.bfloat16)
    v_mix = jnp.dot(tokens, weight_ref[:, 2 * wide :], preferred_element_type=jnp.float32)
    v_ref[...] = jnp.where(lane < span, v_mix + rows[1:2], 0.0).astype(jnp.bfloat16)
    q_mix = jnp.dot(tokens, weight_ref[:, :wide], preferred_element_type=jnp.float32)
    marker = jnp.where(lane == span, 1.0, 0.0)
    q_ref[...] = jnp.where(lane < span, (q_mix + rows[0:1]) * query_scale, marker).astype(jnp.bfloat16)
    keys = k_ref[...]
    tile = min(256, slots)
    for start in range(0, slots, tile):
        total = jnp.zeros((tile, wide), jnp.float32)
        for head in range(heads):
            keep = head_lanes(head, wide)
            q_head = jnp.where(keep | (lane == span), q_ref[start : start + tile, :], 0)
            scores = lax.dot_general(
                q_head, keys, (((1,), (1,)), ((), ())), preferred_element_type=jnp.float32
            )
            peak = jnp.max(scores, axis=-1, keepdims=True)
            raised = jnp.exp(scores - peak)
            summed = jnp.sum(raised, axis=-1, keepdims=True)
            part = jnp.dot(raised.astype(jnp.bfloat16), v_ref[...], preferred_element_type=jnp.float32)
            total = jnp.where(keep, part * (1.0 / summed), total)
            lse_ref[start : start + tile, head : head + 1] = peak + jnp.log(summed)
        att_ref[start : start + tile, :] = total.astype(jnp.bfloat16)


def attend(tokens, weight, rows, key_mask, heads):
    slots = tokens.shape[0]
    wide = weight.shape[1] // 3
    low = jax.ShapeDtypeStruct((slots, wide), jnp.bfloat16)
    return pl.pallas_call(
        partial(attend_kernel, heads=heads),
        out_shape=(low, low, low, low, jax.ShapeDtypeStruct((slots, 128), jnp.float32)),
        name="attend",
    )(tokens, weight, rows, key_mask)


def attend_back_kernel(q_ref, k_ref, v_ref, att_ref, grad_ref, lse_ref, mixed_ref, dk_ref, dv_ref, *, heads):
    span = heads * HEAD
    slots, wide = q_ref.shape
    lane = lax.broadcasted_iota(jnp.int32, (1, wide), 1)
    query_scale = HEAD ** (-0.5)
    tile = min(256, slots)
    over_rows = (((0,), (0,)), ((), ()))
    over_lanes = (((1,), (1,)), ((), ()))
    for start in range(0, slots, tile):
        q_total = jnp.zeros((tile, wide), jnp.float32)
        grads = grad_ref[start : start + tile, :]
        products = grads.astype(jnp.float32) * att_ref[start : start + tile, :].astype(jnp.float32)
        for head in range(heads):
            keep = head_lanes(head, wide)
            q_head = jnp.where(keep | (lane == span), q_ref[start : start + tile, :], 0)
            g_head = jnp.where(keep, grads, 0)
            delta = jnp.sum(jnp.where(keep, products, 0.0), axis=-1, keepdims=True)
            scores = lax.dot_general(q_head, k_ref[...], over_lanes, preferred_element_type=jnp.float32)
            probs = jnp.exp(scores - lse_ref[start : start + tile, head : head + 1])
            prob_grad = lax.dot_general(g_head, v_ref[...], over_lanes, preferred_element_type=jnp.float32)
            score_low = (probs * (prob_grad - delta)).astype(jnp.bfloat16)
            part = jnp.dot(score_low, k_ref[...], preferred_element_type=jnp.float32)
            q_total = jnp.where(keep, part, q_total)
            dk = lax.dot_general(score_low, q_head, over_rows, preferred_element_type=jnp.float32)
            dv = lax.dot_general(probs.astype(jnp.bfloat16), g_head, over_rows, preferred_element_type=jnp.float32)
            if start == 0 and head == 0:
                dk_ref[...] = dk
                dv_ref[...] = dv
            else:
                dk_ref[...] += dk
                dv_ref[...] += dv
        mixed_ref[start : start + tile, :wide] = (q_total.astype(jnp.bfloat16) * query_scale).astype(jnp.bfloat16)
    mixed_ref[:, wide : 2 * wide] = jnp.where(lane < span, dk_ref[...], 0.0).astype(jnp.bfloat16)
    mixed_ref[:, 2 * wide :] = dv_ref[...].astype(jnp.bfloat16)


def attend_back(q_rows, k_rows, v_rows, att, grads, lse, heads):
    slots, wide = q_rows.shape
    return pl.pallas_call(
        partial(attend_back_kernel, heads=heads),
        out_shape=jax.ShapeDtypeStruct((slots, 3 * wide), jnp.bfloat16),
        scratch_shapes=[pltpu.VMEM((slots, wide), jnp.float32), pltpu.VMEM((slots, wide), jnp.float32)],
        name="attend_back",
    )(q_rows, k_rows, v_rows, att, grads, lse)


def pair_columns(own, other, index):
    first = index == 0
    return jnp.concatenate([jnp.where(first, own, other), jnp.where(first, other, own)], axis=-1)


def turn(rows):
    half = rows.shape[0] // 2
    return jnp.concatenate([rows[half:], rows[:half]], axis=0)


def split_body(
    tokens,
    doc_lengths,
    group_deal,
    qkv_weight,
    out_weight,
    up_weight,
    up_bias,
    down_weight,
    proj_weight,
    vectors,
    cotangent,
):
    bf16, f32 = jnp.bfloat16, jnp.float32
    y, x, c, z = (lax.axis_index(name) for name in "yxcz")
    depth = lax.axis_size("z")
    seq_count, group, width = tokens.shape
    ranks = lax.axis_size("x") * lax.axis_size("c")
    rank = 2 * x + c
    heads = H // ranks
    span = heads * HEAD
    wide = 256
    rest = wide - span
    shard = qkv_weight.shape[0]
    ff_shard = down_weight.shape[0]
    half_ff = ff_shard // 2
    half_d = width // 2
    embed = proj_weight.shape[1]
    place = 2 * y + x
    z_bits = [1 << k for k in range(depth.bit_length() - 1)]

    def cut(which):
        return lax.dynamic_slice_in_dim(qkv_weight, which * width + rank * span, span, 1)

    rest_pad = jnp.zeros((shard, rest), bf16)
    first_pack = jnp.concatenate(
        [cut(0), rest_pad, cut(1), proj_weight[:, : embed // 2], cut(2), proj_weight[:, embed // 2 :]],
        axis=1,
    )
    small = jnp.concatenate(
        [
            jnp.pad(vectors, ((0, 0), (0, 3 * wide - shard))),
            up_bias[None, :],
            jnp.zeros((7, 3 * wide), bf16),
        ],
        axis=0,
    )
    first_pack = jnp.concatenate([first_pack, small], axis=0)[None]
    z_order = [0]
    for bit in reversed(z_bits):
        first_pack, z_order = grow(first_pack, z_order, "z", bit, 1)
    qkv_rank, small_rows = place_blocks(
        jnp.stack([z, z]).astype(jnp.int32),
        [first_pack],
        [(0, shard, 0, 3 * wide), (shard, shard + 16, 0, 3 * wide)],
        [z_order, z_order],
    )
    small_rows = small_rows.reshape(depth, 16, 3 * wide)
    head_rows = pick(small_rows, rank)[:8, :wide]
    vector_full = jnp.concatenate([small_rows[k, :8, :shard] for k in range(depth)], axis=1)
    vector_full = vector_full.astype(f32)
    bias_core = lax.dynamic_slice_in_dim(small_rows[:, 8, :], c * half_ff, half_ff, 1).reshape(-1)
    bias_core = bias_core.astype(f32)
    proj_full = jnp.concatenate(
        [qkv_rank[:, wide + span : 2 * wide], qkv_rank[:, 2 * wide + span :]], axis=1
    )

    own_tokens, other_tokens = pick(tokens, y), pick(tokens, 1 - y)
    own_cot, other_cot = pick(cotangent, y), pick(cotangent, 1 - y)
    got = swap(jnp.concatenate([other_tokens, other_cot], axis=1), "y")
    rows_two = jnp.concatenate([own_tokens, got[:, :width]], axis=0)
    cot_two = jnp.concatenate([own_cot, got[:, width:]], axis=0)
    rows_four = jnp.concatenate([rows_two, swap(rows_two, "x")], axis=0)
    rows_all = jnp.concatenate([rows_four, swap(rows_four, "c")], axis=0)
    block = 4 * y + 2 * x + c
    order = jnp.array([0, 4, 2, 6, 1, 5, 3, 7], jnp.int32)
    sequence = z * seq_count + y
    deal = lax.dynamic_index_in_dim(group_deal, sequence, 0, keepdims=False)
    length = lax.dynamic_index_in_dim(doc_lengths, sequence, 0, keepdims=False)
    homes = jnp.bitwise_xor(order, block)
    deal_here = jnp.sum(
        jnp.where(homes[:, None] == jnp.arange(deal.shape[0])[None, :], deal[None, :], 0), axis=1
    )
    positions = (deal_here[:, None] * group + jnp.arange(group, dtype=jnp.int32)[None, :]).reshape(-1)
    valid = positions < length
    slots = valid.shape[0]
    marker = jnp.arange(wide) == span
    key_mask = jnp.where(marker[None, :] & ~valid[:, None], NEG_FILL, 0.0).astype(bf16)
    two = 2 * group
    row_mask = valid[:two].astype(f32)[:, None]

    att, q_rows, k_rows, v_rows, lse = attend(rows_all, qkv_rank, head_rows, key_mask, heads)

    quarter = shard // 4
    up_rows = lax.dynamic_slice_in_dim(up_weight, place * quarter, quarter, 0)
    out_rows = lax.dynamic_slice_in_dim(out_weight, place * quarter, quarter, 0)
    second_pack = jnp.concatenate(
        [
            lax.dynamic_slice_in_dim(up_rows[:, k * ff_shard : (k + 1) * ff_shard], c * half_ff, half_ff, 1)
            for k in range(depth)
        ]
        + [lax.dynamic_slice_in_dim(out_rows, c * half_d, half_d, 1)],
        axis=1,
    )[None]
    down_quarter = half_ff // 4
    third_pack = lax.dynamic_slice_in_dim(
        down_weight, c * half_ff + place * down_quarter, down_quarter, 0
    )[None]
    second_order, third_order = [0], [0]
    for bit in reversed(z_bits):
        second_pack, second_order = grow(second_pack, second_order, "z", bit, 4)
        third_pack, third_order = grow(third_pack, third_order, "z", bit, 4)
    second_pack, second_order = grow(second_pack, second_order, "y", 1, 2)
    third_pack, third_order = grow(third_pack, third_order, "x", 1, 1)
    second_order = second_order + [home ^ 1 for home in second_order]
    third_order = third_order + [home ^ 2 for home in third_order]
    here = 4 * z + place
    hidden = depth * half_ff

    def rank_home(home):
        low = home >> 2
        return (((low & 1) << 1) | (low >> 1)) * 4 + (home & 3)

    out_flip = rank_home(jnp.bitwise_xor(4 * z, 4 * rank)) + place
    up_full, out_full = place_blocks(
        jnp.stack([here, out_flip]).astype(jnp.int32),
        [second_pack, swap(second_pack, "x")],
        [(0, quarter, 0, hidden), (0, quarter, hidden, hidden + half_d)],
        [second_order, [rank_home(home) for home in second_order]],
    )
    (down_full,) = place_blocks(
        here.astype(jnp.int32)[None],
        [third_pack, swap(third_pack, "y")],
        [(0, down_quarter, 0, width)],
        [third_order],
    )

    att = att[:, :span].reshape(2, 2, two, span)
    att_x = swap(att[:, 1].reshape(2 * two, span), "x")
    att_half = jnp.concatenate([att[:, 0].reshape(2 * two, span), att_x], axis=1)
    att_full = jnp.concatenate([att_half, turn(swap(att_half, "c"))], axis=1)
    out_part = jnp.dot(att_full, out_full, preferred_element_type=f32)
    out_rows = pair_columns(out_part[:two], swap(out_part[two:], "c"), c)
    first_sum = rows_two.astype(f32) + (out_rows + vector_full[2])
    normed, unit_one, scale_one = norm_rows(first_sum, vector_full[3], vector_full[4])
    normed_own = normed.astype(bf16)
    normed_low = jnp.concatenate([normed_own, swap(normed_own, "c")], axis=0)
    inner_sum = jnp.dot(normed_low, up_full, preferred_element_type=f32) + bias_core
    active, gelu_slope = gelu_both(inner_sum)
    active_low = active.astype(bf16)
    down_part = jnp.dot(active_low, down_full, preferred_element_type=f32)
    second_sum = normed + (down_part[:two] + swap(down_part[two:], "c") + vector_full[5])
    final_sum, unit_two, scale_two = norm_rows(second_sum, vector_full[6], vector_full[7])
    final_low = final_sum.astype(bf16)
    project = jnp.dot(final_low, proj_full, preferred_element_type=f32)
    inverse = lax.rsqrt(jnp.sum(project * project, axis=-1, keepdims=True) + NORM_EPS)
    direction = project * inverse
    emb_two = (direction * row_mask).astype(bf16)
    emb_other = swap(emb_two[group:], "y")

    upstream = cot_two.astype(f32) * row_mask
    project_grad = (
        inverse * (upstream - direction * jnp.sum(upstream * direction, axis=-1, keepdims=True))
    ).astype(bf16)
    over_rows = (((0,), (0,)), ((), ()))
    over_cols = (((1,), (1,)), ((), ()))

    def rows_dot(left, right):
        return lax.dot_general(left, right, over_rows, preferred_element_type=f32)

    def cols_dot(left, right):
        return lax.dot_general(left, right, over_cols, preferred_element_type=f32)

    proj_grad = rows_dot(final_low, project_grad).astype(bf16)
    final_grad = cols_dot(project_grad, proj_full)
    second_grad, gain_two, shift_two = norm_back_rows(final_grad, unit_two, scale_two, vector_full[6])
    down_own = second_grad.astype(bf16)
    down_low = jnp.concatenate([down_own, swap(down_own, "c")], axis=0)
    down_grad = rows_dot(active_low, down_low).astype(bf16)
    inner_grad = cols_dot(down_low, down_full) * gelu_slope
    bias_grad = jnp.sum(inner_grad, axis=0)
    inner_low = inner_grad.astype(bf16)
    up_grad = rows_dot(normed_low, inner_low).astype(bf16)
    normed_part = cols_dot(inner_low, up_full)
    normed_grad = second_grad + (normed_part[:two] + swap(normed_part[two:], "c"))
    first_grad, gain_one, shift_one = norm_back_rows(normed_grad, unit_one, scale_one, vector_full[3])
    first_low = first_grad.astype(bf16)
    mine = lax.dynamic_slice_in_dim(first_low, c * half_d, half_d, 1)
    theirs = lax.dynamic_slice_in_dim(first_low, (1 - c) * half_d, half_d, 1)
    first_core = jnp.concatenate([mine, swap(theirs, "c")], axis=0)
    att_grad_part = cols_dot(first_core, out_full).astype(bf16)
    half_feat = 2 * span
    att_grad = (
        att_grad_part[:, :half_feat].astype(f32)
        + turn(swap(att_grad_part[:, half_feat:], "c")).astype(f32)
    ).astype(bf16)
    got_grad = swap(att_grad[:, span:], "x").reshape(2, 1, two, span)
    own_grad = att_grad[:, :span].reshape(2, 1, two, span)
    grads_all = jnp.concatenate([own_grad, got_grad], axis=1).reshape(slots, span)
    grads_all = jnp.pad(grads_all, ((0, 0), (0, rest)))
    att_all = jnp.pad(att.reshape(slots, span), ((0, 0), (0, rest)))
    mixed_grad = attend_back(q_rows, k_rows, v_rows, att_all, grads_all, lse, heads)

    out_grad = rows_dot(att_full, first_core).astype(bf16)
    out_grad = out_grad.reshape(2, 2, shard, half_d)
    out_grad = jnp.where(x == 1, out_grad[:, ::-1], out_grad)
    out_grad = jnp.where(c == 1, out_grad[::-1], out_grad)
    out_grad = jnp.swapaxes(out_grad, 0, 1).reshape(width, half_d)

    token_part = cols_dot(mixed_grad, qkv_rank)
    four = slots // 2
    token_four = token_part[:four] + swap(token_part[four:].astype(bf16), "c").astype(f32)
    token_two = token_four[:two] + swap(token_four[two:].astype(bf16), "x").astype(f32) + first_grad
    token_other = swap(token_two[group:].astype(bf16), "y").astype(f32)
    token_own = token_two[:group]
    tokens_grad = jnp.where(y == 0, jnp.stack([token_own, token_other]), jnp.stack([token_other, token_own]))
    emb_own = emb_two[:group]
    embeddings = jnp.where(y == 0, jnp.stack([emb_own, emb_other]), jnp.stack([emb_other, emb_own]))

    def halve(value, axis_name, bit, index, front):
        keep = lax.dynamic_index_in_dim(value, index, front, keepdims=False)
        send = lax.dynamic_index_in_dim(value, 1 - index, front, keepdims=False)
        return (keep.astype(f32) + swap(send, axis_name, bit).astype(f32)).astype(bf16)

    def halve_z(value):
        for bit in z_bits:
            value = value.reshape((value.shape[0] // 2, 2) + value.shape[1:])
            value = halve(value, "z", bit, jnp.bitwise_and(z // bit, 1), 1)
        return value[0]

    def widen(value, axis_name, index, axis):
        other = swap(value, axis_name)
        first = index == 0
        return jnp.concatenate(
            [jnp.where(first, value, other), jnp.where(first, other, value)], axis=axis
        )

    down_sum = down_grad.reshape(depth, 2, 2, down_quarter, width)
    down_sum = halve(down_sum, "y", 1, y, 1)
    down_sum = halve(down_sum, "x", 1, x, 1)
    down_sum = halve_z(down_sum)
    down_sum = widen(widen(down_sum, "x", x, 0), "y", y, 0)
    down_sum = widen(down_sum, "c", c, 0).astype(f32)
    up_sum = jnp.concatenate([up_grad, out_grad], axis=1).reshape(depth, 2, 2, quarter, hidden + half_d)
    up_sum = halve(up_sum, "x", 1, x, 2)
    up_sum = halve(up_sum, "y", 1, y, 1)
    up_sum = halve_z(up_sum)
    up_sum = widen(widen(up_sum, "y", y, 0)[None].reshape(2, 1, quarter, hidden + half_d), "x", x, 1)
    up_sum = up_sum.reshape(shard, hidden + half_d)
    up_other = swap(up_sum, "c")
    first = c == 0
    up_low = jnp.where(first, up_sum, up_other).astype(f32)
    up_high = jnp.where(first, up_other, up_sum).astype(f32)
    up_out = jnp.concatenate(
        [part[:, k * half_ff : (k + 1) * half_ff] for k in range(depth) for part in (up_low, up_high)], axis=1
    )
    out_out = jnp.concatenate([up_low[:, hidden:], up_high[:, hidden:]], axis=1)

    qkv_grad = rows_dot(rows_all, mixed_grad).astype(bf16)
    proj_sum = proj_grad
    qkv_grad = jnp.concatenate(
        [
            qkv_grad[:, : wide + span],
            proj_sum[:, : embed // 2],
            qkv_grad[:, 2 * wide : 2 * wide + span],
            proj_sum[:, embed // 2 :],
        ],
        axis=1,
    )
    column_sums = jnp.sum(mixed_grad.astype(f32), axis=0)

    def at_rank(values):
        return jnp.where(jnp.arange(width) // span == rank, jnp.tile(values, ranks), 0.0)

    vector_grad = jnp.stack(
        [
            at_rank(column_sums[:span]),
            at_rank(column_sums[2 * wide : 2 * wide + span]),
            jnp.sum(first_grad, axis=0),
            gain_one,
            shift_one,
            jnp.sum(second_grad, axis=0),
            gain_two,
            shift_two,
        ],
        axis=0,
    )
    vector_blocks = jnp.swapaxes(vector_grad.reshape(8, depth, shard), 0, 1)
    vector_blocks = jnp.pad(vector_blocks, ((0, 0), (0, 0), (0, 3 * wide - shard)))
    bias_blocks = bias_grad.reshape(depth, 1, half_ff)
    bias_zero = jnp.zeros_like(bias_blocks)
    bias_blocks = jnp.concatenate(
        [jnp.where(first, bias_blocks, bias_zero), jnp.where(first, bias_zero, bias_blocks)], axis=2
    )
    small_blocks = jnp.concatenate(
        [vector_blocks, bias_blocks, jnp.zeros((depth, 7, 3 * wide), f32)], axis=1
    ).astype(bf16)
    last = jnp.concatenate([qkv_grad.reshape(depth, shard, 3 * wide), small_blocks], axis=1)
    last = halve_z(last)
    last = (last.astype(f32) + swap(last, "y").astype(f32)).astype(bf16)
    last_x = swap(last, "x")
    pair_small = (last.astype(f32) + last_x.astype(f32)).astype(bf16)
    low_x = jnp.where(x == 0, last, last_x)
    high_x = jnp.where(x == 0, last_x, last)
    both = jnp.concatenate([low_x[:shard], high_x[:shard], pair_small[shard:]], axis=0)
    proj_half = pair_small[:shard]
    both = jnp.concatenate([both, proj_half], axis=0)
    other = swap(both, "c")
    low_c = jnp.where(first, both, other)
    high_c = jnp.where(first, other, both)
    pieces = []
    for which in range(3):
        for block_x in range(2):
            for source in (low_c, high_c):
                pieces.append(
                    source[block_x * shard : (block_x + 1) * shard, which * wide : which * wide + span]
                )
    qkv_out = jnp.concatenate(pieces, axis=1).astype(f32)
    total_small = both.astype(f32) + other.astype(f32)
    small_total = total_small[2 * shard : 2 * shard + 16].astype(bf16).astype(f32)
    proj_total = total_small[2 * shard + 16 :].astype(bf16).astype(f32)
    proj_out = jnp.concatenate(
        [proj_total[:, wide + span : 2 * wide], proj_total[:, 2 * wide + span :]], axis=1
    )
    vectors_out = small_total[:8, :shard]
    bias_out = small_total[8]
    return (
        embeddings,
        tokens_grad,
        qkv_out,
        out_out,
        up_out,
        bias_out,
        down_sum,
        proj_out,
        vectors_out,
    )


def norm_back_rows(grad_in, unit_rows, scaled, gain_row):
    result, gain_grad, shift_grad = norm_back(grad_in[None], unit_rows[None], scaled[None], gain_row)
    return (result[0], gain_grad, shift_grad)


def splits_evenly(mesh):
    ctx_count, depth = mesh.shape["ctx"], mesh.shape["wa"]
    return ctx_count == 8 and depth & (depth - 1) == 0 and H % (ctx_count // 2) == 0 and depth == ctx_count // 2


def solution(mesh):
    split = splits_evenly(mesh)
    ctx = ("y", "x", "c") if split else "ctx"
    wa = "z" if split else "wa"
    if split:
        mesh = jax.sharding.Mesh(mesh.devices.reshape(2, 2, 2, -1), ("y", "x", "c", "z"))
    in_specs = (
        P(wa, ctx, None),
        P(),
        P(),
        P(wa, None),
        P(wa, None),
        P(wa, None),
        P(wa),
        P(wa, None),
        P(wa, None),
        P(None, wa),
        P(wa, ctx, None),
    )
    out_specs = (
        P(wa, ctx, None),
        P(wa, ctx, None),
        P(wa, None),
        P(wa, None),
        P(wa, None),
        P(wa),
        P(wa, None),
        P(wa, None),
        P(None, wa),
    )
    return jax.shard_map(
        split_body if split else body, mesh=mesh, in_specs=in_specs, out_specs=out_specs, check_vma=False
    )
```
